512 devices in a mesh: strata: 32 (over z, x_lo), shard: 16 (over y, x_hi, core).
Axes of the slice: x: 4 (x_hi: 2, x_lo: 2; x = x_hi * 2 + x_lo), y: 4, z: 16, core: 2. Of those that a mesh axis runs over, the one named last changes fastest.
Arguments:
- user_factors: bfloat16 [524288, 512], P(('strata', 'shard')), may hold values from -1.1953125 to 1.1953125
- item_factors: float32 [16384, 512], P(('strata', 'shard')), may hold values from -1.2 to 1.2
- tile_blocks: int32 [32, 16, 3, 8, 2], P('strata', 'shard'), may hold values from 0 to 7, as said below
- tile_counts: int32 [32, 16, 3], P('strata', 'shard'), may hold values from 1 to 8, as said below
- ratings: bfloat16 [32, 16, 3, 8, 128, 128], P('strata', 'shard'), may hold values from -5 to 5
- mask_words: int32 [32, 16, 3, 8, 16, 128], P('strata', 'shard'), may hold values from 0 to 255
Outputs:
- users_out: bfloat16 [524288, 512], P(('strata', 'shard'))
- items_out: float32 [16384, 512], P(('strata', 'shard'))
The draws below stay inside these ranges and needn't reach their ends.
Inputs may be any that keep to these rules, and one draw needn't show every extreme that they name: `tile_blocks`: entry 0 is a user block below 8, entry 1 an item block below 4; the 8 pairs of one stratum, shard and visit are distinct. `tile_counts`: some stratum, shard and visit has exactly 8 live slots in every draw.
All inputs are finite; a program needn't handle non-finite values.
Results may differ from the reference program's by a relative error of at most 0.0095.
Values may be sent and summed in bfloat16 or wider, within the bound.
A program may use at most 64 MiB of HBM per device.

```python
import jax
import jax.numpy as jnp
from jax import lax

R = 512
TILE = 128
USER_DEV = 1024
P_SIZE = 512
TILES = 8
VISITS = 3
WORDS = 16
USERS = 524288
ITEMS = 16384
N_STRATA = 32
N_SHARD = 16


def draw_tile_blocks(key, part):
    cells = USER_DEV // TILE * (P_SIZE // TILE)
    scores = jax.random.randint(key, (N_STRATA, N_SHARD, VISITS, cells), 0, 1 << 20) * cells
    scores = scores + jnp.arange(cells, dtype=jnp.int32)
    order = jnp.argsort(scores, axis=-1)[..., :TILES].astype(jnp.int32)
    return jnp.stack([order // (P_SIZE // TILE), order % (P_SIZE // TILE)], axis=-1).astype(jnp.int32)


def draw_tile_counts(key, part):
    first, second = jax.random.split(key)
    counts = jax.random.randint(first, (N_STRATA * N_SHARD * VISITS,), 1, TILES + 1)
    spot = jax.random.randint(second, (), 0, N_STRATA * N_SHARD * VISITS)
    counts = jnp.where(jnp.arange(N_STRATA * N_SHARD * VISITS) == spot, TILES, counts)
    return counts.reshape(N_STRATA, N_SHARD, VISITS).astype(jnp.int32)


def draw_mask_words(key, part):
    return jax.random.randint(key, (N_STRATA, N_SHARD, VISITS, TILES, WORDS, TILE), 0, 256).astype(jnp.int32)


def level_of(rng, dims, cuts, low, largest):
    gain = 1.0
    for axis_at, shards_of in cuts:
        heights = jax.random.uniform(jax.random.fold_in(jax.random.fold_in(rng, 6), axis_at), (shards_of,), jnp.float32, low / len(cuts), largest / len(cuts))
        gain = gain * jnp.repeat(jnp.exp(heights), dims[axis_at] // shards_of).reshape((-1,) + (1,) * (len(dims) - 1 - axis_at))
    return gain


def gaussian(own_key, extent, deviation, most, pieces=(), kind=jnp.bfloat16):
    factor_of = level_of(own_key, extent, pieces, -0.22, 0.18) if pieces else 1.0
    values = jax.random.normal(own_key, extent, jnp.float32) * deviation * factor_of
    return jnp.minimum(jnp.maximum(values, -most), most).astype(kind)


def setup_inputs(seed: int = 0) -> dict:
    keys = jax.random.split(jax.random.key(seed), 7)
    user_factors = gaussian(keys[0], (USERS, R), 0.2, 1.1953125, ((0, 512),))
    item_factors = gaussian(keys[1], (ITEMS, R), 0.2, 1.2, ((0, 512),), jnp.float32)
    tile_blocks = draw_tile_blocks(jax.random.fold_in(keys[6], 71), 0)
    tile_counts = draw_tile_counts(jax.random.fold_in(keys[6], 71), 0)
    ratings = gaussian(keys[4], (N_STRATA, N_SHARD, VISITS, TILES, TILE, TILE), 1.0, 5.0, ((0, 32), (1, 16)))
    mask_words = draw_mask_words(jax.random.fold_in(keys[6], 71), 0)
    return dict(user_factors=user_factors, item_factors=item_factors, tile_blocks=tile_blocks, tile_counts=tile_counts, ratings=ratings, mask_words=mask_words)


step_user = 0.05
step_item = 0.004
shrinkage = 0.05


def unpack_mask(words):
    shifts = jnp.arange(8, dtype=jnp.int32)
    bits = jnp.bitwise_and(jnp.right_shift(words[:, :, None, :], shifts[None, None, :, None]), 1)
    return bits.reshape(words.shape[0], words.shape[1] * 8, words.shape[2]).astype(jnp.float32)


def device_terms(user_part, panel_part, blocks, count, rates, words):
    tile_side = rates.shape[-1]
    width = user_part.shape[1]
    user_blocks = user_part.reshape(-1, tile_side, width)
    item_blocks = panel_part.reshape(-1, tile_side, width)
    user_rows = jnp.take(user_blocks, blocks[:, 0], axis=0).astype(jnp.float32)
    item_rows = jnp.take(item_blocks, blocks[:, 1], axis=0).astype(jnp.float32)
    predicted = jnp.einsum('kur,kir->kui', user_rows, item_rows)
    live = (jnp.arange(blocks.shape[0], dtype=jnp.int32) < count).astype(jnp.float32)
    weights = unpack_mask(words) * live[:, None, None]
    error_tile = (weights * (rates.astype(jnp.float32) - predicted)).astype(jnp.bfloat16).astype(jnp.float32)
    user_terms = jnp.einsum('kui,kir->kur', error_tile, item_rows)
    item_terms = jnp.einsum('kui,kur->kir', error_tile, user_rows)
    user_hot = (blocks[:, 0][:, None] == jnp.arange(user_blocks.shape[0], dtype=jnp.int32)[None, :]).astype(jnp.float32)
    item_hot = (blocks[:, 1][:, None] == jnp.arange(item_blocks.shape[0], dtype=jnp.int32)[None, :]).astype(jnp.float32)
    grad_user = jnp.einsum('kb,kur->bur', user_hot, user_terms).reshape(-1, width)
    grad_item = jnp.einsum('kb,kir->bir', item_hot, item_terms).reshape(-1, width)
    return grad_user, grad_item.astype(jnp.bfloat16)


def reference(user_factors, item_factors, tile_blocks, tile_counts, ratings, mask_words):
    users = user_factors.reshape(N_STRATA, N_SHARD, USER_DEV, R)
    panels = item_factors.reshape(N_STRATA, P_SIZE, R)
    for visit in range(VISITS):
        current = jnp.roll(panels, visit, axis=0)
        panel_low = current.astype(jnp.bfloat16)

        def stratum_terms(packed):
            user_part, panel_part, blocks, counts, rates, words = packed
            grad_user, grad_item = jax.vmap(device_terms, in_axes=(0, None, 0, 0, 0, 0))(
                user_part, panel_part, blocks, counts, rates, words)
            return grad_user, jnp.sum(grad_item.astype(jnp.float32), axis=0)

        grad_users, grad_items = lax.map(stratum_terms, (users, panel_low, tile_blocks[:, :, visit],
                                                         tile_counts[:, :, visit], ratings[:, :, visit],
                                                         mask_words[:, :, visit]))
        factor = users.astype(jnp.float32)
        users = (factor + step_user * (grad_users - shrinkage * factor)).astype(jnp.bfloat16)
        current = current + step_item * (grad_items - shrinkage * current)
        panels = jnp.roll(current, -visit, axis=0)
    return users.reshape(-1, R), jnp.roll(panels, VISITS - 1, axis=0).reshape(-1, R)
```

```python
import jax
import jax.numpy as jnp
from jax import lax
from jax.experimental import pallas as pl
from jax.experimental.pallas import tpu as pltpu
from jax.sharding import PartitionSpec as P

MESH = pl.DeviceIdType.MESH
BF = jnp.bfloat16
F32 = jnp.float32

step_user = 0.05
step_item = 0.004
shrinkage = 0.05

NY, NX, NC = 4, 2, 2
T, K, SIDE, R = 3, 8, 128, 512
J, W = 2, 256
PIECE = 32
UB, IB = 8, 4
N_STRATA = 32


def kernel(
    blocks, counts, users_in, items, ratings_in, words_in,
    users_out, items_out,
    users, ratings, words, panel, err, err_t, dense, dense_t, grads,
    c_out, c_in, y_out, y_in, x_out, x_in, f_out, f_in,
    load_sem, c_send, c_recv, y_send, y_recv, x_send, x_recv, f_send, f_recv,
    g_send, g_recv, p_send, p_recv, i_send, i_recv,
):
    s = lax.axis_index("strata")
    h = lax.axis_index("shard")
    y = h // 4
    x = (h // 2) % 2
    c = h % 2
    after = lax.rem(s + 1, N_STRATA)
    before = lax.rem(s + N_STRATA - 1, N_STRATA)

    def shard_of(yy, xx, cc):
        return yy * 4 + xx * 2 + cc

    def row(dy):
        return lax.rem(y + dy, NY)

    mate = (s, shard_of(y, x, 1 - c))

    loads = [
        pltpu.make_async_copy(users_in, users, load_sem.at[0]),
        pltpu.make_async_copy(ratings_in, ratings, load_sem.at[1]),
        pltpu.make_async_copy(words_in, words, load_sem.at[2]),
    ]
    for load in loads:
        load.start()

    barrier = pltpu.get_barrier_semaphore()
    partners = [mate, (s, shard_of(y, 1 - x, c))]
    partners += [(s, shard_of(row(dy), x, c)) for dy in (1, 2, 3)]
    partners += [(after, shard_of(y, xx, c)) for xx in range(NX)]
    partners += [(before, shard_of(y, xx, c)) for xx in range(NX)]
    for partner in partners:
        pl.semaphore_signal(barrier, inc=1, device_id=partner, device_id_type=MESH)

    for j in range(J):
        panel[0, j, y, x, c] = items[:, j * W:(j + 1) * W].astype(BF)

    pl.semaphore_wait(barrier, len(partners))

    def remote(src, dst, send, recv, to):
        return pltpu.make_async_remote_copy(
            src_ref=src, dst_ref=dst, send_sem=send, recv_sem=recv, device_id=to, device_id_type=MESH
        )

    def first_copy(j, xx):
        part = panel.at[0, j, y, xx, c]
        return remote(part, part, i_send.at[j], i_recv.at[j], (s, shard_of(y, 1 - x, c)))

    def gather_y(t, j, dy, yy):
        part = panel.at[t, j, yy, :, c]
        return remote(part, part, g_send.at[t, j, dy - 1], g_recv.at[t, j, dy - 1], (s, shard_of(row(dy), x, c)))

    def gather_c(t, j, dy, cc):
        part = panel.at[t, j, row(4 - dy), :, cc]
        return remote(part, part, p_send.at[t, j, dy], p_recv.at[t, j, dy], mate)

    def reduce_c(t, j):
        return remote(c_out.at[t, j], c_in.at[t, j], c_send.at[t, j], c_recv.at[t, j], mate)

    def reduce_y(t, j, dy):
        return remote(
            y_out.at[t, j, dy - 1], y_in.at[t, j, dy - 1], y_send.at[t, j, dy - 1], y_recv.at[t, j, dy - 1],
            (s, shard_of(row(dy), x, c)),
        )

    def advance(t, j, xx, slot):
        return remote(
            x_out.at[t, j], x_in.at[t, j, slot], x_send.at[t, j, xx], x_recv.at[t, j, slot],
            (after, shard_of(y, xx, c)),
        )

    def last_copy(j):
        return remote(f_out.at[j], f_in.at[j], f_send.at[j], f_recv.at[j], (s, shard_of(y, 1 - x, c)))

    def gather_start(t, j):
        for dy in (2, 1, 3):
            gather_y(t, j, dy, y).start()
        gather_c(t, j, 0, c).start()

    def gather_finish(t):
        for j in range(J):
            for dy in (1, 3, 2):
                gather_y(t, j, dy, row(4 - dy)).wait_recv()
                gather_c(t, j, dy, c).start()
        for j in range(J):
            for dy in range(NY):
                gather_c(t, j, dy, 1 - c).wait_recv()

    for j in range(J):
        first_copy(j, x).start()

    def slots_of(t):
        cells = [blocks[t * 2 * K + 2 * k] * IB + blocks[t * 2 * K + 2 * k + 1] for k in range(K)]
        found = []
        for cell in range(UB * IB):
            rank = (cells[0] == cell).astype(jnp.int32) * K
            for k in range(1, K):
                rank = jnp.maximum(rank, (cells[k] == cell).astype(jnp.int32) * (K - k))
            found.append(K - rank)
        return found

    err[K] = jnp.zeros((SIDE, SIDE), BF)
    err_t[K] = jnp.zeros((SIDE, SIDE), BF)

    for j in range(J):
        first_copy(j, 1 - x).wait_recv()
        gather_start(0, j)
    for load in loads:
        load.wait()
    gather_finish(0)

    bit = lax.broadcasted_iota(jnp.int32, (16, 8, SIDE), 1)

    def tile_error(t, k):
        at = blocks[t * 2 * K + 2 * k]
        item = blocks[t * 2 * K + 2 * k + 1]
        live = (k < counts[t]).astype(jnp.int32)
        predicted = jnp.zeros((SIDE, SIDE), F32)
        for j in range(J):
            rows = panel[t, j, item].reshape(SIDE, W)
            predicted += lax.dot_general(
                users[at, :, j * W:(j + 1) * W], rows, (((1,), (1,)), ((), ())), preferred_element_type=F32
            )
        mask = jnp.bitwise_and(jnp.right_shift(words[t * K + k][:, None, :], bit), live).reshape(SIDE, SIDE)
        error = jnp.where(mask != 0, ratings[t * K + k].astype(F32) - predicted, 0.0)
        err[k] = error.astype(BF)
        err_t[k] = error.T.astype(BF)

    def reduce_pair(t, j):
        for dy in (2, 1, 3):
            yy = row(dy)
            y_out[t, j, dy - 1] = (grads[j, yy, :, c] + c_in[t, j, yy].astype(F32)).astype(BF)
            reduce_y(t, j, dy).start()

    def reduced(t, j):
        total = grads[j, y, :, c] + c_in[t, j, y].astype(F32)
        for dy in (1, 3, 2):
            reduce_y(t, j, dy).wait_recv()
            total += y_in[t, j, dy - 1].astype(F32)
        return total

    def update_users(t, j):
        columns = slice(j * W, (j + 1) * W)
        grad = jnp.dot(dense[...], panel[t, j].reshape(IB * SIDE, W), preferred_element_type=F32)
        grad = grad.reshape(UB, SIDE, W)
        factor = users[:, :, columns].astype(F32)
        users[:, :, columns] = (factor + step_user * (grad - shrinkage * factor)).astype(BF)

    def visit(t, last):
        for k in range(K):
            tile_error(t, k)
        slots = slots_of(t)
        for b in range(IB):
            for a in range(UB):
                slot = slots[a * IB + b]
                dense_t[b * SIDE:(b + 1) * SIDE, a * SIDE:(a + 1) * SIDE] = err_t[slot]
        for j in range(J):
            grads[j] = jnp.dot(
                dense_t[...], users[:, :, j * W:(j + 1) * W].reshape(UB * SIDE, W), preferred_element_type=F32
            ).reshape(NY, NX, NC, PIECE, W)
            c_out[t, j] = grads[j, :, :, 1 - c].astype(BF)
            reduce_c(t, j).start()
        for b in range(IB):
            for a in range(UB):
                slot = slots[a * IB + b]
                dense[a * SIDE:(a + 1) * SIDE, b * SIDE:(b + 1) * SIDE] = err[slot]
        for j in range(J):
            reduce_c(t, j).wait_recv()
            reduce_pair(t, j)
        update_users(t, 0)
        if not last:
            for j in range(J):
                total = reduced(t, j)
                mine = panel[t, j, y, :, c].astype(F32)
                half = step_item * total + (0.5 * (1.0 - step_item * shrinkage)) * mine
                x_out[t, j] = half.astype(BF)
                for xx in range(NX):
                    advance(t, j, xx, x).start()
            update_users(t, 1)
            for j in range(J):
                for xx in range(NX):
                    advance(t, j, xx, xx).wait_recv()
                both = x_in[t, j, 0].astype(F32) + x_in[t, j, 1].astype(F32)
                panel[t + 1, j, y, :, c] = both.astype(BF)
                gather_start(t + 1, j)
            gather_finish(t + 1)
        else:
            for j in range(J):
                grads[j, y, :, c] = reduced(t, j)
                f_out[j] = grads[j, y, 1 - x, c].astype(BF)
                last_copy(j).start()
            update_users(t, 1)
            out = pltpu.make_async_copy(users, users_out, load_sem.at[0])
            out.start()
            for j in range(J):
                last_copy(j).wait_recv()
                total = grads[j, y, x, c] + f_in[j].astype(F32)
                mine = panel[t, j, y, x, c].astype(F32)
                items_out[:, j * W:(j + 1) * W] = mine + step_item * (total - shrinkage * mine)
            out.wait()

    for t in range(T):
        visit(t, t == T - 1)

    for j in range(J):
        first_copy(j, x).wait_send()
        last_copy(j).wait_send()
        for t in range(T):
            reduce_c(t, j).wait_send()
            for dy in (1, 2, 3):
                reduce_y(t, j, dy).wait_send()
                gather_y(t, j, dy, y).wait_send()
            for dy in range(NY):
                gather_c(t, j, dy, c).wait_send()
            if t < T - 1:
                for xx in range(NX):
                    advance(t, j, xx, x).wait_send()


def shards(user_factors, item_factors, tile_blocks, tile_counts, ratings, mask_words):
    dma = pltpu.SemaphoreType.DMA
    vmem = pltpu.VMEM
    space = pl.BlockSpec(memory_space=pl.ANY)
    users, panel = pl.pallas_call(
        kernel,
        out_shape=(
            jax.ShapeDtypeStruct((UB, SIDE, R), BF),
            jax.ShapeDtypeStruct((PIECE, R), F32),
        ),
        in_specs=[
            pl.BlockSpec(memory_space=pltpu.SMEM),
            pl.BlockSpec(memory_space=pltpu.SMEM),
            space,
            pl.BlockSpec(memory_space=pltpu.VMEM),
            space,
            space,
        ],
        out_specs=(space, pl.BlockSpec(memory_space=pltpu.VMEM)),
        scratch_shapes=[
            vmem((UB, SIDE, R), BF),
            vmem((T * K, SIDE, SIDE), BF),
            vmem((T * K, SIDE // 8, SIDE), jnp.int32),
            vmem((T, J, NY, NX, NC, PIECE, W), BF),
            vmem((K + 1, SIDE, SIDE), BF),
            vmem((K + 1, SIDE, SIDE), BF),
            vmem((UB * SIDE, IB * SIDE), BF),
            vmem((IB * SIDE, UB * SIDE), BF),
            vmem((J, NY, NX, NC, PIECE, W), F32),
            vmem((T, J, NY, NX, PIECE, W), BF),
            vmem((T, J, NY, NX, PIECE, W), BF),
            vmem((T, J, 3, NX, PIECE, W), BF),
            vmem((T, J, 3, NX, PIECE, W), BF),
            vmem((T - 1, J, NX, PIECE, W), BF),
            vmem((T - 1, J, NX, NX, PIECE, W), BF),
            vmem((J, PIECE, W), BF),
            vmem((J, PIECE, W), BF),
            dma((3,)),
            dma((T, J)), dma((T, J)),
            dma((T, J, 3)), dma((T, J, 3)),
            dma((T - 1, J, NX)), dma((T - 1, J, NX)),
            dma((J,)), dma((J,)),
            dma((T, J, 3)), dma((T, J, 3)),
            dma((T, J, NY)), dma((T, J, NY)),
            dma((J,)), dma((J,)),
        ],
        compiler_params=pltpu.CompilerParams(
            collective_id=0, has_side_effects=True, vmem_limit_bytes=60 * 1024 * 1024
        ),
    )(
        tile_blocks.reshape(T * K * 2),
        tile_counts.reshape(T),
        user_factors.reshape(UB, SIDE, R),
        item_factors,
        ratings.reshape(T * K, SIDE, SIDE),
        mask_words.reshape(T * K, SIDE // 8, SIDE),
    )
    return users.reshape(UB * SIDE, R), panel


def solution(mesh):
    placed = (
        P(("strata", "shard"), None),
        P(("strata", "shard"), None),
        P("strata", "shard", None, None, None),
        P("strata", "shard", None),
        P("strata", "shard", None, None, None, None),
        P("strata", "shard", None, None, None, None),
    )
    return jax.shard_map(
        shards,
        mesh=mesh,
        in_specs=placed,
        out_specs=(P(("strata", "shard"), None), P(("strata", "shard"), None)),
        check_vma=False,
    )
```

```python
import jax
import jax.numpy as jnp
from jax import lax
from jax.experimental import pallas as pl
from jax.experimental.pallas import tpu as pltpu
from jax.sharding import PartitionSpec as P

MESH = pl.DeviceIdType.MESH
BF = jnp.bfloat16
F32 = jnp.float32

step_user = 0.05
step_item = 0.004
shrinkage = 0.05

NY, NX, NC = 4, 2, 2
T, K, SIDE, R = 3, 8, 128, 512
J, W = 2, 256
PIECE = 32
UB, IB = 8, 4
N_STRATA = 32
H = 2
PART = PIECE // H
Q = J * H
PEERS = [(2, 1), (1, 1), (3, 1), (2, 0), (0, 1), (1, 0), (3, 0)]


def kernel(
    blocks_in, counts_in, users_in, items_in, ratings_in, words_in,
    users_out, items_out,
    blocks, counts, users, items, ratings, words, panel, err, err_t, dense, dense_t, grads,
    c_out, c_in, y_out, y_in, x_out, x_in, r_out, r_in,
    load_sem, c_send, c_recv, y_send, y_recv, x_send, x_recv, r_send, r_recv,
    g_send, g_recv, p_send, p_recv, i_send, i_recv, k_send, k_recv,
):
    s = lax.axis_index("strata")
    h = lax.axis_index("shard")
    y = h // 4
    x = (h // 2) % 2
    c = h % 2
    after = lax.rem(s + 1, N_STRATA)
    before = lax.rem(s + N_STRATA - 1, N_STRATA)

    def row(dy):
        return lax.rem(y + dy, NY)

    def at(dy, dx, cc):
        return row(dy) * 4 + (1 - x if dx else x) * 2 + cc

    mate = (s, at(0, 0, 1 - c))

    barrier = pltpu.get_barrier_semaphore()
    partners = [mate] + [(s, at(dy, dx, c)) for dy, dx in PEERS]
    partners += [(after, y * 4 + xx * 2 + c) for xx in range(NX)]
    partners += [(before, y * 4 + xx * 2 + c) for xx in range(NX)]
    for partner in partners:
        pl.semaphore_signal(barrier, inc=1, device_id=partner, device_id_type=MESH)

    first_load = pltpu.make_async_copy(items_in, items, load_sem.at[3])
    first_load.start()
    loads = [
        pltpu.make_async_copy(users_in, users, load_sem.at[0]),
        pltpu.make_async_copy(ratings_in, ratings, load_sem.at[1]),
        pltpu.make_async_copy(words_in, words, load_sem.at[2]),
        pltpu.make_async_copy(blocks_in, blocks, load_sem.at[4]),
        pltpu.make_async_copy(counts_in, counts, load_sem.at[5]),
    ]
    for load in loads:
        load.start()

    first_load.wait()
    for j in range(J):
        panel[0, j, y, x, c] = items[:, j * W:(j + 1) * W].astype(BF)

    pl.semaphore_wait(barrier, len(partners))

    def remote(src, dst, send, recv, to):
        return pltpu.make_async_remote_copy(
            src_ref=src, dst_ref=dst, send_sem=send, recv_sem=recv, device_id=to, device_id_type=MESH
        )

    def first_copy(i, yy, xx):
        part = panel.at[0, :, yy, xx, c]
        dy, dx = PEERS[i]
        return remote(part, part, i_send.at[i], i_recv.at[i], (s, at(dy, dx, c)))

    def first_pair(i, yy, xx, cc):
        part = panel.at[0, :, yy, xx, cc]
        return remote(part, part, k_send.at[i], k_recv.at[i], mate)

    def rows_of(q):
        return pl.ds((q % H) * PART, PART)

    def gather_y(t, q, dy, yy):
        part = panel.at[t, q // H, yy, :, c, rows_of(q)]
        return remote(part, part, g_send.at[t - 1, q, dy - 1], g_recv.at[t - 1, q, dy - 1], (s, at(dy, 0, c)))

    def gather_c(t, q, dy, cc):
        part = panel.at[t, q // H, row(4 - dy), :, cc, rows_of(q)]
        return remote(part, part, p_send.at[t - 1, q, dy], p_recv.at[t - 1, q, dy], mate)

    def reduce_c(t, q):
        return remote(c_out.at[t, q], c_in.at[t, q], c_send.at[t, q], c_recv.at[t, q], mate)

    def reduce_y(t, q, dy):
        return remote(
            y_out.at[t, q, dy - 1], y_in.at[t, q, dy - 1], y_send.at[t, q, dy - 1], y_recv.at[t, q, dy - 1],
            (s, at(dy, 0, c)),
        )

    def advance(t, q, xx, slot):
        return remote(
            x_out.at[t, q], x_in.at[t, q, slot], x_send.at[t, q, xx], x_recv.at[t, q, slot],
            (after, y * 4 + xx * 2 + c),
        )

    def reduce_last(j, i):
        dy, dx = PEERS[i]
        return remote(r_out.at[j, i], r_in.at[j, i], r_send.at[j, i], r_recv.at[j, i], (s, at(dy, dx, c)))

    for i in range(len(PEERS)):
        first_copy(i, y, x).start()
    first_pair(len(PEERS), y, x, c).start()
    err[K] = jnp.zeros((SIDE, SIDE), BF)
    err_t[K] = jnp.zeros((SIDE, SIDE), BF)
    for i in reversed(range(len(PEERS))):
        dy, dx = PEERS[i]
        yy, xx = row(4 - dy), (1 - x if dx else x)
        first_copy(i, yy, xx).wait_recv()
        first_pair(i, yy, xx, c).start()
    for load in loads:
        load.wait()
    for i, (dy, dx) in enumerate(PEERS + [(0, 0)]):
        first_pair(i, row(4 - dy), (1 - x if dx else x), 1 - c).wait_recv()

    def slots_of(t):
        cells = [blocks[t, 0, k] * IB + blocks[t, 1, k] for k in range(K)]
        found = []
        for cell in range(UB * IB):
            rank = (cells[0] == cell).astype(jnp.int32) * K
            for k in range(1, K):
                rank = jnp.maximum(rank, (cells[k] == cell).astype(jnp.int32) * (K - k))
            found.append(K - rank)
        return found

    bit = lax.broadcasted_iota(jnp.int32, (16, 8, SIDE), 1)

    def tile_error(t, k):
        a = blocks[t, 0, k]
        b = blocks[t, 1, k]
        live = (k < counts[t]).astype(jnp.int32)
        predicted = jnp.zeros((SIDE, SIDE), F32)
        for j in range(J):
            rows = panel[t, j, b].reshape(SIDE, W)
            predicted += lax.dot_general(
                users[a, :, j * W:(j + 1) * W], rows, (((1,), (1,)), ((), ())), preferred_element_type=F32
            )
        mask = jnp.bitwise_and(jnp.right_shift(words[t * K + k][:, None, :], bit), live).reshape(SIDE, SIDE)
        error = jnp.where(mask != 0, ratings[t * K + k].astype(F32) - predicted, 0.0)
        err[k] = error.astype(BF)
        err_t[k] = error.T.astype(BF)

    def update_users(t, j):
        columns = slice(j * W, (j + 1) * W)
        grad = jnp.dot(dense[...], panel[t, j].reshape(IB * SIDE, W), preferred_element_type=F32)
        grad = grad.reshape(UB, SIDE, W)
        factor = users[:, :, columns].astype(F32)
        users[:, :, columns] = (factor + step_user * (grad - shrinkage * factor)).astype(BF)

    def paired(t, q, yy, xx=slice(None)):
        mine = grads[q // H, yy, xx, c, (q % H) * PART:(q % H + 1) * PART]
        return mine + c_in[t, q, yy, xx].astype(F32)

    for t in range(T):
        for k in range(K):
            tile_error(t, k)
        slots = slots_of(t)
        for b in range(IB):
            for a in range(UB):
                dense_t[b * SIDE:(b + 1) * SIDE, a * SIDE:(a + 1) * SIDE] = err_t[slots[a * IB + b]]
        for j in range(J):
            grads[j] = jnp.dot(
                dense_t[...], users[:, :, j * W:(j + 1) * W].reshape(UB * SIDE, W), preferred_element_type=F32
            ).reshape(NY, NX, NC, PIECE, W)
            for q in range(j * H, (j + 1) * H):
                c_out[t, q] = grads[j, :, :, 1 - c, (q % H) * PART:(q % H + 1) * PART].astype(BF)
                reduce_c(t, q).start()
        for b in range(IB):
            for a in range(UB):
                dense[a * SIDE:(a + 1) * SIDE, b * SIDE:(b + 1) * SIDE] = err[slots[a * IB + b]]
        if t < T - 1:
            for q in range(Q):
                reduce_c(t, q).wait_recv()
                for dy in (2, 1, 3):
                    y_out[t, q, dy - 1] = paired(t, q, row(dy)).astype(BF)
                    reduce_y(t, q, dy).start()
            for j in range(J):
                update_users(t, j)
            for q in range(Q):
                total = paired(t, q, y)
                for dy in (1, 3, 2):
                    reduce_y(t, q, dy).wait_recv()
                    total += y_in[t, q, dy - 1].astype(F32)
                mine = panel[t, q // H, y, :, c, (q % H) * PART:(q % H + 1) * PART].astype(F32)
                half = step_item * total + (0.5 * (1.0 - step_item * shrinkage)) * mine
                x_out[t, q] = half.astype(BF)
                for xx in range(NX):
                    advance(t, q, xx, x).start()
            for q in range(Q):
                for xx in range(NX):
                    advance(t, q, xx, xx).wait_recv()
                both = x_in[t, q, 0].astype(F32) + x_in[t, q, 1].astype(F32)
                panel[t + 1, q // H, y, :, c, (q % H) * PART:(q % H + 1) * PART] = both.astype(BF)
                for dy in (2, 1, 3):
                    gather_y(t + 1, q, dy, y).start()
                gather_c(t + 1, q, 0, c).start()
            for q in range(Q):
                for dy in (1, 3, 2):
                    gather_y(t + 1, q, dy, row(4 - dy)).wait_recv()
                    gather_c(t + 1, q, dy, c).start()
            for q in range(Q):
                for dy in range(NY):
                    gather_c(t + 1, q, dy, 1 - c).wait_recv()
        else:
            for j in range(J):
                for q in range(j * H, (j + 1) * H):
                    reduce_c(t, q).wait_recv()
                for i, (dy, dx) in enumerate(PEERS):
                    for q in range(j * H, (j + 1) * H):
                        part = paired(t, q, row(dy), 1 - x if dx else x)
                        r_out[j, i, (q % H) * PART:(q % H + 1) * PART] = part.astype(BF)
                    reduce_last(j, i).start()
            for j in range(J):
                update_users(t, j)
            out = pltpu.make_async_copy(users, users_out, load_sem.at[0])
            out.start()
            for j in range(J):
                own = [paired(t, q, y, x) for q in range(j * H, (j + 1) * H)]
                total = jnp.concatenate(own, axis=0)
                for i in reversed(range(len(PEERS))):
                    reduce_last(j, i).wait_recv()
                    total += r_in[j, i].astype(F32)
                mine = panel[t, j, y, x, c].astype(F32)
                items[:, j * W:(j + 1) * W] = mine + step_item * (total - shrinkage * mine)
            last = pltpu.make_async_copy(items, items_out, load_sem.at[1])
            last.start()

    for i in range(len(PEERS)):
        first_copy(i, y, x).wait_send()
        first_pair(i, y, x, c).wait_send()
        for j in range(J):
            reduce_last(j, i).wait_send()
    first_pair(len(PEERS), y, x, c).wait_send()
    for q in range(Q):
        for t in range(T):
            reduce_c(t, q).wait_send()
        for t in range(T - 1):
            for dy in (1, 2, 3):
                reduce_y(t, q, dy).wait_send()
                gather_y(t + 1, q, dy, y).wait_send()
            for dy in range(NY):
                gather_c(t + 1, q, dy, c).wait_send()
            for xx in range(NX):
                advance(t, q, xx, x).wait_send()
    out.wait()
    last.wait()


def shards(user_factors, item_factors, tile_blocks, tile_counts, ratings, mask_words):
    dma = pltpu.SemaphoreType.DMA
    vmem = pltpu.VMEM
    space = pl.BlockSpec(memory_space=pl.ANY)
    fixed = pl.BlockSpec(memory_space=pltpu.HBM)
    n = len(PEERS)

    def far(a):
        return pltpu.with_memory_space_constraint(a, pltpu.HBM)

    users, panel = pl.pallas_call(
        kernel,
        out_shape=(
            jax.ShapeDtypeStruct((UB, SIDE, R), BF),
            jax.ShapeDtypeStruct((PIECE, R), F32),
        ),
        in_specs=[
            fixed,
            fixed,
            fixed,
            fixed,
            fixed,
            fixed,
        ],
        out_specs=(space, space),
        scratch_shapes=[
            pltpu.SMEM((T, 2, K), jnp.int32),
            pltpu.SMEM((T,), jnp.int32),
            vmem((UB, SIDE, R), BF),
            vmem((PIECE, R), F32),
            vmem((T * K, SIDE, SIDE), BF),
            vmem((T * K, SIDE // 8, SIDE), jnp.int32),
            vmem((T, J, NY, NX, NC, PIECE, W), BF),
            vmem((K + 1, SIDE, SIDE), BF),
            vmem((K + 1, SIDE, SIDE), BF),
            vmem((UB * SIDE, IB * SIDE), BF),
            vmem((IB * SIDE, UB * SIDE), BF),
            vmem((J, NY, NX, NC, PIECE, W), F32),
            vmem((T, Q, NY, NX, PART, W), BF),
            vmem((T, Q, NY, NX, PART, W), BF),
            vmem((T - 1, Q, 3, NX, PART, W), BF),
            vmem((T - 1, Q, 3, NX, PART, W), BF),
            vmem((T - 1, Q, NX, PART, W), BF),
            vmem((T - 1, Q, NX, NX, PART, W), BF),
            vmem((J, n, PIECE, W), BF),
            vmem((J, n, PIECE, W), BF),
            dma((6,)),
            dma((T, Q)), dma((T, Q)),
            dma((T - 1, Q, 3)), dma((T - 1, Q, 3)),
            dma((T - 1, Q, NX)), dma((T - 1, Q, NX)),
            dma((J, n)), dma((J, n)),
            dma((T - 1, Q, 3)), dma((T - 1, Q, 3)),
            dma((T - 1, Q, NY)), dma((T - 1, Q, NY)),
            dma((n,)), dma((n,)),
            dma((n + 1,)), dma((n + 1,)),
        ],
        compiler_params=pltpu.CompilerParams(
            collective_id=0, has_side_effects=True, vmem_limit_bytes=24 * 1024 * 1024
        ),
    )(
        far(tile_blocks.reshape(T, K, 2).transpose(0, 2, 1)),
        far(tile_counts.reshape(T)),
        far(user_factors.reshape(UB, SIDE, R)),
        far(item_factors),
        far(ratings.reshape(T * K, SIDE, SIDE)),
        far(mask_words.reshape(T * K, SIDE // 8, SIDE)),
    )
    return users.reshape(UB * SIDE, R), panel


def solution(mesh):
    placed = (
        P(("strata", "shard"), None),
        P(("strata", "shard"), None),
        P("strata", "shard", None, None, None),
        P("strata", "shard", None),
        P("strata", "shard", None, None, None, None),
        P("strata", "shard", None, None, None, None),
    )
    return jax.shard_map(
        shards,
        mesh=mesh,
        in_specs=placed,
        out_specs=(P(("strata", "shard"), None), P(("strata", "shard"), None)),
        check_vma=False,
    )
```

```python
import jax
import jax.numpy as jnp
from jax import lax
from jax.experimental import pallas as pl
from jax.experimental.pallas import tpu as pltpu
from jax.sharding import PartitionSpec as P

MESH = pl.DeviceIdType.MESH
BF = jnp.bfloat16
F32 = jnp.float32

step_user = 0.05
step_item = 0.004
shrinkage = 0.05

NY, NX, NC = 4, 2, 2
T, K, SIDE, R = 3, 8, 128, 512
J, W = 2, 256
PIECE = 32
UB, IB = 8, 4
N_STRATA = 32
H = 2
PART = PIECE // H
Q = J * H
MARK = 1e30
LIMIT = 1e20
PEERS = [(2, 1), (1, 1), (3, 1), (2, 0), (0, 1), (1, 0), (3, 0)]


def kernel(
    blocks_in, counts_in, users_in, items_in, ratings_in, words_in,
    users_out, items_out,
    blocks, counts, users, items, ratings, words, marked, panel0, panels, predicted, err_t, dense_t, grads,
    u_own, u_out, u_in, y_out, y_in, x_out, x_in, r_out, r_in,
    load_sem, pair_send, pair_recv, u_send, u_recv, n_send, n_recv, y_send, y_recv, x_send, x_recv,
    r_send, r_recv, g_send, g_recv, i_send, i_recv,
):
    s = lax.axis_index("strata")
    h = lax.axis_index("shard")
    y = h // 4
    x = (h // 2) % 2
    c = h % 2
    after = lax.rem(s + 1, N_STRATA)
    before = lax.rem(s + N_STRATA - 1, N_STRATA)

    def row(dy):
        return lax.rem(y + dy, NY)

    def at(dy, dx, cc):
        return row(dy) * 4 + (1 - x if dx else x) * 2 + cc

    mate = (s, at(0, 0, 1 - c))

    barrier = pltpu.get_barrier_semaphore()
    partners = [mate] + [(s, at(dy, dx, c)) for dy, dx in PEERS]
    partners += [(after, y * 4 + xx * 2 + c) for xx in range(NX)]
    partners += [(before, y * 4 + xx * 2 + c) for xx in range(NX)]
    for partner in partners:
        pl.semaphore_signal(barrier, inc=1, device_id=partner, device_id_type=MESH)

    first_load = pltpu.make_async_copy(items_in, items, load_sem.at[0])
    first_load.start()
    pairs = [(blocks_in, blocks), (counts_in, counts), (ratings_in, ratings), (words_in, words), (users_in, users)]
    loads = [pltpu.make_async_copy(src, dst.at[0], load_sem.at[n + 1]) for n, (src, dst) in enumerate(pairs)]
    for load in loads:
        load.start()

    first_load.wait()
    for j in range(J):
        panel0[j, y, x] = items[:, j * W:(j + 1) * W].astype(BF)

    pl.semaphore_wait(barrier, len(partners))

    def remote(src, dst, send, recv, to):
        return pltpu.make_async_remote_copy(
            src_ref=src, dst_ref=dst, send_sem=send, recv_sem=recv, device_id=to, device_id_type=MESH
        )

    def panel_at(t, j, *index):
        return panels[t - 1][j][index] if t else panel0[(j, *index)]

    def first_copy(i, yy, xx):
        part = panel0.at[:, yy, xx]
        dy, dx = PEERS[i]
        return remote(part, part, i_send.at[i], i_recv.at[i], (s, at(dy, dx, c)))

    def share(n):
        src, dst = pairs[n]
        return remote(src, dst.at[1], pair_send.at[n], pair_recv.at[n], mate)

    def rows_of(q):
        return pl.ds((q % H) * PART, PART)

    def gather_y(t, q, dy, yy):
        part = panels[t - 1][q // H].at[yy, :, rows_of(q)]
        return remote(part, part, g_send.at[t - 1, q, dy - 1], g_recv.at[t - 1, q, dy - 1], (s, at(dy, 0, c)))

    def reduce_y(t, q, dy):
        return remote(
            y_out.at[t, q, dy - 1], y_in.at[t, q, dy - 1], y_send.at[t, q, dy - 1], y_recv.at[t, q, dy - 1],
            (s, at(dy, 0, c)),
        )

    def advance(t, q, xx, slot):
        return remote(
            x_out.at[t, q], x_in.at[t, q, slot], x_send.at[t, q, xx], x_recv.at[t, q, slot],
            (after, y * 4 + xx * 2 + c),
        )

    def reduce_last(j, i):
        dy, dx = PEERS[i]
        return remote(r_out.at[j, i], r_in.at[j, i], r_send.at[j, i], r_recv.at[j, i], (s, at(dy, dx, c)))

    def user_grads(t):
        return remote(u_out.at[t], u_in.at[t], u_send.at[t], u_recv.at[t], mate)

    def new_users(t):
        return remote(users.at[0], users.at[1], n_send.at[t], n_recv.at[t], mate)

    bit = lax.broadcasted_iota(jnp.int32, (16, 8, SIDE), 1)

    def mark(t, cc):
        for k in range(K):
            live = (k < counts[cc, t]).astype(jnp.int32)
            mask = jnp.bitwise_and(jnp.right_shift(words[cc, t * K + k][:, None, :], bit), live).reshape(SIDE, SIDE)
            rate = jnp.where(mask != 0, ratings[cc, t * K + k].astype(F32), MARK)
            marked[cc * K + k] = rate.T.astype(BF).reshape(NX, NC, PIECE, SIDE)

    def slots_of(t):
        found = []
        for cc in range(NC):
            cells = [blocks[cc, t, 0, k] * IB + blocks[cc, t, 1, k] for k in range(K)]
            for cell in range(UB * IB):
                rank = (cells[0] == cell).astype(jnp.int32) * (2 * K - cc * K)
                for k in range(1, K):
                    rank = jnp.maximum(rank, (cells[k] == cell).astype(jnp.int32) * (2 * K - cc * K - k))
                found.append(2 * K - rank)
        return found

    def product(t, j, cc, k):
        rows = panel_at(t, j, blocks[cc, t, 1, k]).reshape(NX * PIECE, W)
        return lax.dot_general(
            rows, users[cc, blocks[cc, t, 0, k], :, j * W:(j + 1) * W], (((1,), (1,)), ((), ())),
            preferred_element_type=F32,
        )

    def predict_first(t):
        for cc in range(NC):
            for k in range(K):
                predicted[cc * K + k] = product(t, 0, cc, k)

    def errors(t):
        for cc in range(NC):
            for k in range(K):
                value = predicted[cc * K + k] + product(t, 1, cc, k)
                rate = marked[cc * K + k, :, c].reshape(NX * PIECE, SIDE).astype(F32)
                err_t[cc * K + k] = jnp.where(rate < LIMIT, rate - value, 0.0).astype(BF)

    def user_grad(t, cc, j):
        return lax.dot_general(
            dense_t[:, cc * UB * SIDE:(cc + 1) * UB * SIDE], panel_at(t, j, slice(None)).reshape(NY * NX * PIECE, W),
            (((0,), (0,)), ((), ())), preferred_element_type=F32,
        ).reshape(UB, SIDE, W)

    def columns(j):
        return slice(j * W, (j + 1) * W)

    def send_user_grads(t):
        for j in range(J):
            u_out[t, :, :, columns(j)] = user_grad(t, 1, j).astype(BF)
        user_grads(t).start()
        for j in range(J):
            u_own[:, :, columns(j)] = user_grad(t, 0, j)

    def update_users(t):
        user_grads(t).wait_recv()
        if t > 0:
            new_users(t - 1).wait_send()
        for j in range(J):
            grad = u_own[:, :, columns(j)] + u_in[t, :, :, columns(j)].astype(F32)
            factor = users[0, :, :, columns(j)].astype(F32)
            users[0, :, :, columns(j)] = (factor + step_user * (grad - shrinkage * factor)).astype(BF)

    for i in range(len(PEERS)):
        first_copy(i, y, x).start()
    for n in range(len(pairs)):
        share(n).start()
    err_t[2 * K] = jnp.zeros((NX * PIECE, SIDE), BF)
    for load in loads:
        load.wait()
    mark(0, 0)
    for n in range(len(pairs)):
        share(n).wait_recv()
    mark(0, 1)
    slots = slots_of(0)
    for i, (dy, dx) in enumerate(PEERS):
        first_copy(i, row(4 - dy), (1 - x if dx else x)).wait_recv()
    predict_first(0)

    for t in range(T):
        errors(t)
        for cc in range(NC):
            for b in range(IB):
                for a in range(UB):
                    lanes = slice((cc * UB + a) * SIDE, (cc * UB + a + 1) * SIDE)
                    dense_t[b * NX * PIECE:(b + 1) * NX * PIECE, lanes] = err_t[slots[(cc * UB + a) * IB + b]]
        for j in range(J):
            grads[j] = jnp.dot(
                dense_t[...], users[:, :, :, columns(j)].reshape(NC * UB * SIDE, W), preferred_element_type=F32
            ).reshape(NY, NX, PIECE, W)
            if t < T - 1:
                for q in range(j * H, (j + 1) * H):
                    for dy in (2, 1, 3):
                        y_out[t, q, dy - 1] = grads[j, row(dy), :, (q % H) * PART:(q % H + 1) * PART].astype(BF)
                        reduce_y(t, q, dy).start()
            else:
                for i, (dy, dx) in enumerate(PEERS):
                    r_out[j, i] = grads[j, row(dy), 1 - x if dx else x].astype(BF)
                    reduce_last(j, i).start()
        send_user_grads(t)
        if t < T - 1:
            for q in range(Q):
                total = grads[q // H, y, :, (q % H) * PART:(q % H + 1) * PART]
                for dy in (1, 3, 2):
                    reduce_y(t, q, dy).wait_recv()
                    total += y_in[t, q, dy - 1].astype(F32)
                mine = panel_at(t, q // H, y, slice(None), slice((q % H) * PART, (q % H + 1) * PART)).astype(F32)
                half = step_item * total + (0.5 * (1.0 - step_item * shrinkage)) * mine
                x_out[t, q] = half.astype(BF)
                for xx in range(NX):
                    advance(t, q, xx, x).start()
            update_users(t)
            new_users(t).start()
            for q in range(Q):
                for xx in range(NX):
                    advance(t, q, xx, xx).wait_recv()
                both = x_in[t, q, 0].astype(F32) + x_in[t, q, 1].astype(F32)
                panels[t][q // H][y, :, (q % H) * PART:(q % H + 1) * PART] = both.astype(BF)
                for dy in (2, 1, 3):
                    gather_y(t + 1, q, dy, y).start()
            for cc in range(NC):
                mark(t + 1, cc)
            slots = slots_of(t + 1)
            new_users(t).wait_recv()
            for q in range(H):
                for dy in (1, 3, 2):
                    gather_y(t + 1, q, dy, row(4 - dy)).wait_recv()
            predict_first(t + 1)
            for q in range(H, Q):
                for dy in (1, 3, 2):
                    gather_y(t + 1, q, dy, row(4 - dy)).wait_recv()
        else:
            update_users(t)
            out = pltpu.make_async_copy(users.at[0], users_out, load_sem.at[0])
            out.start()
            for j in range(J):
                total = grads[j, y, x]
                for i in reversed(range(len(PEERS))):
                    reduce_last(j, i).wait_recv()
                    total += r_in[j, i].astype(F32)
                mine = panel_at(t, j, y, x).astype(F32)
                items[:, columns(j)] = mine + step_item * (total - shrinkage * mine)
            last = pltpu.make_async_copy(items, items_out, load_sem.at[1])
            last.start()

    for n in range(len(pairs)):
        share(n).wait_send()
    for i in range(len(PEERS)):
        first_copy(i, y, x).wait_send()
        for j in range(J):
            reduce_last(j, i).wait_send()
    for t in range(T):
        user_grads(t).wait_send()
    for t in range(T - 1):
        for q in range(Q):
            for dy in (1, 2, 3):
                reduce_y(t, q, dy).wait_send()
                gather_y(t + 1, q, dy, y).wait_send()
            for xx in range(NX):
                advance(t, q, xx, x).wait_send()
    out.wait()
    last.wait()


def shards(user_factors, item_factors, tile_blocks, tile_counts, ratings, mask_words):
    dma = pltpu.SemaphoreType.DMA
    vmem = pltpu.VMEM
    space = pl.BlockSpec(memory_space=pl.ANY)
    n = len(PEERS)

    def far(a):
        return pltpu.with_memory_space_constraint(a, pltpu.HBM)

    users, panel = pl.pallas_call(
        kernel,
        out_shape=(
            jax.ShapeDtypeStruct((UB, SIDE, R), BF),
            jax.ShapeDtypeStruct((PIECE, R), F32),
        ),
        in_specs=[pl.BlockSpec(memory_space=pltpu.HBM)] * 6,
        out_specs=(space, space),
        scratch_shapes=[
            pltpu.SMEM((NC, T, 2, K), jnp.int32),
            pltpu.SMEM((NC, T), jnp.int32),
            vmem((NC, UB, SIDE, R), BF),
            vmem((PIECE, R), F32),
            vmem((NC, T * K, SIDE, SIDE), BF),
            vmem((NC, T * K, SIDE // 8, SIDE), jnp.int32),
            vmem((NC * K, NX, NC, PIECE, SIDE), BF),
            vmem((J, NY, NX, PIECE, W), BF),
            [[vmem((NY, NX, PIECE, W), BF) for j in range(J)] for t in range(T - 1)],
            vmem((NC * K, NX * PIECE, SIDE), F32),
            vmem((NC * K + 1, NX * PIECE, SIDE), BF),
            vmem((NY * NX * PIECE, NC * UB * SIDE), BF),
            vmem((J, NY, NX, PIECE, W), F32),
            vmem((UB, SIDE, R), F32),
            vmem((T, UB, SIDE, R), BF),
            vmem((T, UB, SIDE, R), BF),
            vmem((T - 1, Q, 3, NX, PART, W), BF),
            vmem((T - 1, Q, 3, NX, PART, W), BF),
            vmem((T - 1, Q, NX, PART, W), BF),
            vmem((T - 1, Q, NX, NX, PART, W), BF),
            vmem((J, n, PIECE, W), BF),
            vmem((J, n, PIECE, W), BF),
            dma((6,)),
            dma((5,)), dma((5,)),
            dma((T,)), dma((T,)),
            dma((T - 1,)), dma((T - 1,)),
            dma((T - 1, Q, 3)), dma((T - 1, Q, 3)),
            dma((T - 1, Q, NX)), dma((T - 1, Q, NX)),
            dma((J, n)), dma((J, n)),
            dma((T - 1, Q, 3)), dma((T - 1, Q, 3)),
            dma((n,)), dma((n,)),
        ],
        compiler_params=pltpu.CompilerParams(
            collective_id=0, has_side_effects=True, vmem_limit_bytes=36 * 1024 * 1024
        ),
    )(
        far(tile_blocks.reshape(T, K, 2).transpose(0, 2, 1)),
        far(tile_counts.reshape(T)),
        far(user_factors.reshape(UB, SIDE, R)),
        far(item_factors),
        far(ratings.reshape(T * K, SIDE, SIDE)),
        far(mask_words.reshape(T * K, SIDE // 8, SIDE)),
    )
    return users.reshape(UB * SIDE, R), panel


def solution(mesh):
    placed = (
        P(("strata", "shard"), None),
        P(("strata", "shard"), None),
        P("strata", "shard", None, None, None),
        P("strata", "shard", None),
        P("strata", "shard", None, None, None, None),
        P("strata", "shard", None, None, None, None),
    )
    return jax.shard_map(
        shards,
        mesh=mesh,
        in_specs=placed,
        out_specs=(P(("strata", "shard"), None), P(("strata", "shard"), None)),
        check_vma=False,
    )
```

```python
import jax
import jax.numpy as jnp
from jax import lax
from jax.experimental import pallas as pl
from jax.experimental.pallas import tpu as pltpu
from jax.sharding import PartitionSpec as P

MESH = pl.DeviceIdType.MESH
BF = jnp.bfloat16
F32 = jnp.float32

step_user = 0.05
step_item = 0.004
shrinkage = 0.05

NY, NX, NC = 4, 2, 2
T, K, SIDE, R = 3, 8, 128, 512
J, W = 2, 256
PIECE = 32
UB, IB = 8, 4
N_STRATA = 32
H = 2
PART = PIECE // H
Q = J * H
MARK = 1e30
LIMIT = 1e20
PEERS = [(2, 1), (1, 1), (3, 1), (2, 0), (0, 1), (1, 0), (3, 0)]


def kernel(
    blocks_in, counts_in, users_in, items_in, ratings_in, words_in,
    users_out, items_out,
    blocks, counts, users, items, ratings, words, marked, rates, panel0, panels, remaining, dense_t, grads,
    u_own, u_out, u_in, y_out, y_in, x_out, x_in, r_out, r_in,
    load_sem, pair_send, pair_recv, u_send, u_recv, n_send, n_recv, y_send, y_recv, x_send, x_recv,
    r_send, r_recv, g_send, g_recv, i_send, i_recv,
):
    s = lax.axis_index("strata")
    h = lax.axis_index("shard")
    y = h // 4
    x = (h // 2) % 2
    c = h % 2
    after = lax.rem(s + 1, N_STRATA)
    before = lax.rem(s + N_STRATA - 1, N_STRATA)

    def row(dy):
        return lax.rem(y + dy, NY)

    def at(dy, dx, cc):
        return row(dy) * 4 + (1 - x if dx else x) * 2 + cc

    mate = (s, at(0, 0, 1 - c))

    barrier = pltpu.get_barrier_semaphore()
    partners = [mate] + [(s, at(dy, dx, c)) for dy, dx in PEERS]
    partners += [(after, y * 4 + xx * 2 + c) for xx in range(NX)]
    partners += [(before, y * 4 + xx * 2 + c) for xx in range(NX)]
    for partner in partners:
        pl.semaphore_signal(barrier, inc=1, device_id=partner, device_id_type=MESH)

    first_load = pltpu.make_async_copy(items_in, items, load_sem.at[0])
    first_load.start()
    pairs = [(blocks_in, blocks), (counts_in, counts), (ratings_in, ratings), (words_in, words), (users_in, users)]
    loads = [pltpu.make_async_copy(src, dst.at[0], load_sem.at[n + 1]) for n, (src, dst) in enumerate(pairs)]
    for load in loads:
        load.start()

    first_load.wait()
    for j in range(J):
        panel0[j, y, x] = items[:, j * W:(j + 1) * W].astype(BF)

    pl.semaphore_wait(barrier, len(partners))

    def remote(src, dst, send, recv, to):
        return pltpu.make_async_remote_copy(
            src_ref=src, dst_ref=dst, send_sem=send, recv_sem=recv, device_id=to, device_id_type=MESH
        )

    def panel_at(t, j, *index):
        return panels[t - 1][j][index] if t else panel0[(j, *index)]

    def first_copy(i, yy, xx):
        part = panel0.at[:, yy, xx]
        dy, dx = PEERS[i]
        return remote(part, part, i_send.at[i], i_recv.at[i], (s, at(dy, dx, c)))

    def share(n):
        src, dst = pairs[n]
        return remote(src, dst.at[1], pair_send.at[n], pair_recv.at[n], mate)

    def rows_of(q):
        return pl.ds((q % H) * PART, PART)

    def gather_y(t, q, dy, yy):
        part = panels[t - 1][q // H].at[yy, :, rows_of(q)]
        return remote(part, part, g_send.at[t - 1, q, dy - 1], g_recv.at[t - 1, q, dy - 1], (s, at(dy, 0, c)))

    def reduce_y(t, q, dy):
        return remote(
            y_out.at[t, q, dy - 1], y_in.at[t, q, dy - 1], y_send.at[t, q, dy - 1], y_recv.at[t, q, dy - 1],
            (s, at(dy, 0, c)),
        )

    def advance(t, q, xx, slot):
        return remote(
            x_out.at[t, q], x_in.at[t, q, slot], x_send.at[t, q, xx], x_recv.at[t, q, slot],
            (after, y * 4 + xx * 2 + c),
        )

    def reduce_last(j, i):
        dy, dx = PEERS[i]
        return remote(r_out.at[j, i], r_in.at[j, i], r_send.at[j, i], r_recv.at[j, i], (s, at(dy, dx, c)))

    def user_grads(t):
        return remote(u_out.at[t], u_in.at[t], u_send.at[t], u_recv.at[t], mate)

    def new_users(t):
        return remote(users.at[0], users.at[1], n_send.at[t], n_recv.at[t], mate)

    def columns(j):
        return slice(j * W, (j + 1) * W)

    bit = lax.broadcasted_iota(jnp.int32, (16, 8, SIDE), 1)

    def mark(t, cc):
        for k in range(K):
            live = (k < counts[cc, t]).astype(jnp.int32)
            mask = jnp.bitwise_and(jnp.right_shift(words[cc, t * K + k][:, None, :], bit), live).reshape(SIDE, SIDE)
            rate = jnp.where(mask != 0, ratings[cc, t * K + k].astype(F32), MARK)
            marked[cc * K + k] = rate.T.astype(BF).reshape(NX, NC, PIECE, SIDE)

    def slots_of(t):
        found = []
        for cc in range(NC):
            cells = [blocks[cc, t, 0, k] * IB + blocks[cc, t, 1, k] for k in range(K)]
            for cell in range(UB * IB):
                rank = (cells[0] == cell).astype(jnp.int32) * (2 * K - cc * K)
                for k in range(1, K):
                    rank = jnp.maximum(rank, (cells[k] == cell).astype(jnp.int32) * (2 * K - cc * K - k))
                found.append(2 * K - rank)
        return found

    def place(t):
        slots = slots_of(t)
        for cc in range(NC):
            for b in range(IB):
                for a in range(UB):
                    lanes = slice((cc * UB + a) * SIDE, (cc * UB + a + 1) * SIDE)
                    tile = marked[slots[(cc * UB + a) * IB + b], :, c]
                    rates[b * NX * PIECE:(b + 1) * NX * PIECE, lanes] = tile.reshape(NX * PIECE, SIDE)

    def product(t, j, n):
        cc, a = divmod(2 * n, UB)
        return lax.dot_general(
            panel_at(t, j, slice(None)).reshape(NY * NX * PIECE, W),
            users[cc, a:a + 2, :, columns(j)].reshape(2 * SIDE, W),
            (((1,), (1,)), ((), ())), preferred_element_type=F32,
        )

    def group(n):
        return slice(n * 2 * SIDE, (n + 1) * 2 * SIDE)

    def predict_first(t):
        for n in range(UB):
            remaining[n] = rates[:, group(n)].astype(F32) - product(t, 0, n)

    def errors(t):
        for n in range(UB):
            rest = remaining[n]
            dense_t[:, group(n)] = jnp.where(rest < LIMIT, rest - product(t, 1, n), 0.0).astype(BF)

    def user_grad(t, cc, j):
        return lax.dot_general(
            dense_t[:, cc * UB * SIDE:(cc + 1) * UB * SIDE], panel_at(t, j, slice(None)).reshape(NY * NX * PIECE, W),
            (((0,), (0,)), ((), ())), preferred_element_type=F32,
        ).reshape(UB, SIDE, W)

    def send_user_grads(t):
        for j in range(J):
            u_out[t, :, :, columns(j)] = user_grad(t, 1, j).astype(BF)
        user_grads(t).start()
        for j in range(J):
            u_own[:, :, columns(j)] = user_grad(t, 0, j)

    def update_users(t):
        user_grads(t).wait_recv()
        if t > 0:
            new_users(t - 1).wait_send()
        for j in range(J):
            grad = u_own[:, :, columns(j)] + u_in[t, :, :, columns(j)].astype(F32)
            factor = users[0, :, :, columns(j)].astype(F32)
            users[0, :, :, columns(j)] = (factor + step_user * (grad - shrinkage * factor)).astype(BF)

    for i in range(len(PEERS)):
        first_copy(i, y, x).start()
    for n in range(len(pairs)):
        share(n).start()
    marked[2 * K] = jnp.full((NX, NC, PIECE, SIDE), MARK, BF)
    for load in loads:
        load.wait()
    mark(0, 0)
    for n in range(len(pairs)):
        share(n).wait_recv()
    mark(0, 1)
    place(0)
    for i, (dy, dx) in enumerate(PEERS):
        first_copy(i, row(4 - dy), (1 - x if dx else x)).wait_recv()
    predict_first(0)

    for t in range(T):
        errors(t)
        for j in range(J):
            grads[j] = jnp.dot(
                dense_t[...], users[:, :, :, columns(j)].reshape(NC * UB * SIDE, W), preferred_element_type=F32
            ).reshape(NY, NX, PIECE, W)
            if t < T - 1:
                for q in range(j * H, (j + 1) * H):
                    for dy in (2, 1, 3):
                        y_out[t, q, dy - 1] = grads[j, row(dy), :, (q % H) * PART:(q % H + 1) * PART].astype(BF)
                        reduce_y(t, q, dy).start()
            else:
                for i, (dy, dx) in enumerate(PEERS):
                    r_out[j, i] = grads[j, row(dy), 1 - x if dx else x].astype(BF)
                    reduce_last(j, i).start()
        send_user_grads(t)
        if t < T - 1:
            for q in range(Q):
                total = grads[q // H, y, :, (q % H) * PART:(q % H + 1) * PART]
                for dy in (1, 3, 2):
                    reduce_y(t, q, dy).wait_recv()
                    total += y_in[t, q, dy - 1].astype(F32)
                mine = panel_at(t, q // H, y, slice(None), slice((q % H) * PART, (q % H + 1) * PART)).astype(F32)
                half = step_item * total + (0.5 * (1.0 - step_item * shrinkage)) * mine
                x_out[t, q] = half.astype(BF)
                for xx in range(NX):
                    advance(t, q, xx, x).start()
            update_users(t)
            new_users(t).start()
            for q in range(Q):
                for xx in range(NX):
                    advance(t, q, xx, xx).wait_recv()
                both = x_in[t, q, 0].astype(F32) + x_in[t, q, 1].astype(F32)
                panels[t][q // H][y, :, (q % H) * PART:(q % H + 1) * PART] = both.astype(BF)
                for dy in (2, 1, 3):
                    gather_y(t + 1, q, dy, y).start()
            for cc in range(NC):
                mark(t + 1, cc)
            place(t + 1)
            new_users(t).wait_recv()
            for q in range(H):
                for dy in (1, 3, 2):
                    gather_y(t + 1, q, dy, row(4 - dy)).wait_recv()
            predict_first(t + 1)
            for q in range(H, Q):
                for dy in (1, 3, 2):
                    gather_y(t + 1, q, dy, row(4 - dy)).wait_recv()
        else:
            update_users(t)
            out = pltpu.make_async_copy(users.at[0], users_out, load_sem.at[0])
            out.start()
            for j in range(J):
                total = grads[j, y, x]
                for i in reversed(range(len(PEERS))):
                    reduce_last(j, i).wait_recv()
                    total += r_in[j, i].astype(F32)
                mine = panel_at(t, j, y, x).astype(F32)
                items[:, columns(j)] = mine + step_item * (total - shrinkage * mine)
            last = pltpu.make_async_copy(items, items_out, load_sem.at[1])
            last.start()

    for n in range(len(pairs)):
        share(n).wait_send()
    for i in range(len(PEERS)):
        first_copy(i, y, x).wait_send()
        for j in range(J):
            reduce_last(j, i).wait_send()
    for t in range(T):
        user_grads(t).wait_send()
    for t in range(T - 1):
        for q in range(Q):
            for dy in (1, 2, 3):
                reduce_y(t, q, dy).wait_send()
                gather_y(t + 1, q, dy, y).wait_send()
            for xx in range(NX):
                advance(t, q, xx, x).wait_send()
    out.wait()
    last.wait()


def store(users_in, items_in, users_out, items_out, sem):
    copies = [
        pltpu.make_async_copy(users_in, users_out, sem.at[0]),
        pltpu.make_async_copy(items_in, items_out, sem.at[1]),
    ]
    for copy in copies:
        copy.start()
    for copy in copies:
        copy.wait()


def shards(user_factors, item_factors, tile_blocks, tile_counts, ratings, mask_words):
    dma = pltpu.SemaphoreType.DMA
    vmem = pltpu.VMEM
    space = pl.BlockSpec(memory_space=pl.ANY)
    n = len(PEERS)

    def far(a):
        return pltpu.with_memory_space_constraint(a, pltpu.HBM)

    users, panel = pl.pallas_call(
        kernel,
        out_shape=(
            jax.ShapeDtypeStruct((UB, SIDE, R), BF),
            jax.ShapeDtypeStruct((PIECE, R), F32),
        ),
        in_specs=[pl.BlockSpec(memory_space=pltpu.HBM)] * 6,
        out_specs=(space, space),
        scratch_shapes=[
            pltpu.SMEM((NC, T, 2, K), jnp.int32),
            pltpu.SMEM((NC, T), jnp.int32),
            vmem((NC, UB, SIDE, R), BF),
            vmem((PIECE, R), F32),
            vmem((NC, T * K, SIDE, SIDE), BF),
            vmem((NC, T * K, SIDE // 8, SIDE), jnp.int32),
            vmem((NC * K + 1, NX, NC, PIECE, SIDE), BF),
            vmem((NY * NX * PIECE, NC * UB * SIDE), BF),
            vmem((J, NY, NX, PIECE, W), BF),
            [[vmem((NY, NX, PIECE, W), BF) for j in range(J)] for t in range(T - 1)],
            vmem((UB, NY * NX * PIECE, 2 * SIDE), F32),
            vmem((NY * NX * PIECE, NC * UB * SIDE), BF),
            vmem((J, NY, NX, PIECE, W), F32),
            vmem((UB, SIDE, R), F32),
            vmem((T, UB, SIDE, R), BF),
            vmem((T, UB, SIDE, R), BF),
            vmem((T - 1, Q, 3, NX, PART, W), BF),
            vmem((T - 1, Q, 3, NX, PART, W), BF),
            vmem((T - 1, Q, NX, PART, W), BF),
            vmem((T - 1, Q, NX, NX, PART, W), BF),
            vmem((J, n, PIECE, W), BF),
            vmem((J, n, PIECE, W), BF),
            dma((6,)),
            dma((5,)), dma((5,)),
            dma((T,)), dma((T,)),
            dma((T - 1,)), dma((T - 1,)),
            dma((T - 1, Q, 3)), dma((T - 1, Q, 3)),
            dma((T - 1, Q, NX)), dma((T - 1, Q, NX)),
            dma((J, n)), dma((J, n)),
            dma((T - 1, Q, 3)), dma((T - 1, Q, 3)),
            dma((n,)), dma((n,)),
        ],
        compiler_params=pltpu.CompilerParams(
            collective_id=0, has_side_effects=True, vmem_limit_bytes=36 * 1024 * 1024
        ),
    )(
        far(tile_blocks.reshape(T, K, 2).transpose(0, 2, 1)),
        far(tile_counts.reshape(T)),
        far(user_factors.reshape(UB, SIDE, R)),
        far(item_factors),
        far(ratings.reshape(T * K, SIDE, SIDE)),
        far(mask_words.reshape(T * K, SIDE // 8, SIDE)),
    )
    users, panel = pl.pallas_call(
        store,
        out_shape=(
            jax.ShapeDtypeStruct((UB, SIDE, R), BF),
            jax.ShapeDtypeStruct((PIECE, R), F32),
        ),
        in_specs=[space] * 2,
        out_specs=(pl.BlockSpec(memory_space=pltpu.HBM),) * 2,
        scratch_shapes=[dma((2,))],
        compiler_params=pltpu.CompilerParams(vmem_limit_bytes=1024 * 1024),
    )(users, panel)
    return users.reshape(UB * SIDE, R), panel


def solution(mesh):
    placed = (
        P(("strata", "shard"), None),
        P(("strata", "shard"), None),
        P("strata", "shard", None, None, None),
        P("strata", "shard", None),
        P("strata", "shard", None, None, None, None),
        P("strata", "shard", None, None, None, None),
    )
    return jax.shard_map(
        shards,
        mesh=mesh,
        in_specs=placed,
        out_specs=(P(("strata", "shard"), None), P(("strata", "shard"), None)),
        check_vma=False,
    )
```

```python
import jax
import jax.numpy as jnp
from jax import lax
from jax.experimental import pallas as pl
from jax.experimental.pallas import tpu as pltpu
from jax.sharding import PartitionSpec as P

MESH = pl.DeviceIdType.MESH
BF = jnp.bfloat16
F32 = jnp.float32

step_user = 0.05
step_item = 0.004
shrinkage = 0.05

NY, NX, NC = 4, 2, 2
T, K, SIDE, R = 3, 8, 128, 512
J, W = 2, 256
PIECE = 32
UB, IB = 8, 4
N_STRATA = 32
MARK = 1e30
LIMIT = 1e20
PEERS = [(2, 1), (1, 1), (3, 1), (2, 0), (0, 1), (1, 0), (3, 0)]
NEXT = [(2, 1), (2, 0), (1, 1), (1, 0), (3, 1), (3, 0), (0, 1), (0, 0)]


def kernel(
    blocks_in, counts_in, users_in, items_in, ratings_in, words_in,
    users_out, items_out,
    blocks, counts, users, items, ratings, words, marked, rates, panel0, panels, remaining, dense_t, grads,
    u_own, u_out, u_in, a_out, r_out, r_in,
    load_sem, pair_send, pair_recv, u_send, u_recv, n_send, n_recv, a_send, a_recv, r_send, r_recv, i_send, i_recv,
):
    s = lax.axis_index("strata")
    h = lax.axis_index("shard")
    y = h // 4
    x = (h // 2) % 2
    c = h % 2
    after = lax.rem(s + 1, N_STRATA)
    before = lax.rem(s + N_STRATA - 1, N_STRATA)

    def row(dy):
        return lax.rem(y + dy, NY)

    def at(dy, dx, cc):
        return row(dy) * 4 + (1 - x if dx else x) * 2 + cc

    mate = (s, at(0, 0, 1 - c))

    barrier = pltpu.get_barrier_semaphore()
    partners = [mate] + [(s, at(dy, dx, c)) for dy, dx in PEERS]
    partners += [(after, row(dy) * 4 + xx * 2 + c) for dy, xx in NEXT]
    partners += [(before, row(dy) * 4 + xx * 2 + c) for dy, xx in NEXT]
    for partner in partners:
        pl.semaphore_signal(barrier, inc=1, device_id=partner, device_id_type=MESH)

    first_load = pltpu.make_async_copy(items_in, items, load_sem.at[0])
    first_load.start()
    pairs = [(blocks_in, blocks), (counts_in, counts), (ratings_in, ratings), (words_in, words), (users_in, users)]
    loads = [pltpu.make_async_copy(src, dst.at[0], load_sem.at[n + 1]) for n, (src, dst) in enumerate(pairs)]
    for load in loads:
        load.start()

    first_load.wait()
    for j in range(J):
        panel0[j, y, x] = items[:, j * W:(j + 1) * W].astype(BF)

    pl.semaphore_wait(barrier, len(partners))

    def remote(src, dst, send, recv, to):
        return pltpu.make_async_remote_copy(
            src_ref=src, dst_ref=dst, send_sem=send, recv_sem=recv, device_id=to, device_id_type=MESH
        )

    def panel_at(t, j, *index):
        return panels[t - 1][j][index] if t else panel0[(j, *index)]

    def first_copy(i, yy, xx):
        part = panel0.at[:, yy, xx]
        dy, dx = PEERS[i]
        return remote(part, part, i_send.at[i], i_recv.at[i], (s, at(dy, dx, c)))

    def share(n):
        src, dst = pairs[n]
        return remote(src, dst.at[1], pair_send.at[n], pair_recv.at[n], mate)

    def reduce(t, j, i):
        dy, dx = PEERS[i]
        return remote(r_out.at[t, j, i], r_in.at[t, j, i], r_send.at[t, j], r_recv.at[t, j], (s, at(dy, dx, c)))

    def reduce_all(t, j):
        return remote(r_out.at[t, j], r_in.at[t, j], r_send.at[t, j], r_recv.at[t, j], mate)

    def advance(t, j, i):
        dy, xx = NEXT[i]
        return remote(
            a_out.at[t, j], panels[t][j].at[y, x], a_send.at[t, j, i], a_recv.at[t, j],
            (after, row(dy) * 4 + xx * 2 + c),
        )

    def advance_all(t, j):
        return remote(panels[t][j], panels[t][j], a_send.at[t, j, 0], a_recv.at[t, j], mate)

    def user_grads(t):
        return remote(u_out.at[t], u_in.at[t], u_send.at[t], u_recv.at[t], mate)

    def new_users(t):
        return remote(users.at[0], users.at[1], n_send.at[t], n_recv.at[t], mate)

    def columns(j):
        return slice(j * W, (j + 1) * W)

    bit = lax.broadcasted_iota(jnp.int32, (16, 8, SIDE), 1)

    def mark(t, cc):
        for k in range(K):
            live = (k < counts[cc, t]).astype(jnp.int32)
            mask = jnp.bitwise_and(jnp.right_shift(words[cc, t * K + k][:, None, :], bit), live).reshape(SIDE, SIDE)
            rate = jnp.where(mask != 0, ratings[cc, t * K + k].astype(F32), MARK)
            marked[cc * K + k] = rate.T.astype(BF).reshape(NX, NC, PIECE, SIDE)

    def slots_of(t):
        found = []
        for cc in range(NC):
            cells = [blocks[cc, t, 0, k] * IB + blocks[cc, t, 1, k] for k in range(K)]
            for cell in range(UB * IB):
                rank = (cells[0] == cell).astype(jnp.int32) * (2 * K - cc * K)
                for k in range(1, K):
                    rank = jnp.maximum(rank, (cells[k] == cell).astype(jnp.int32) * (2 * K - cc * K - k))
                found.append(2 * K - rank)
        return found

    def place(t):
        slots = slots_of(t)
        for cc in range(NC):
            for b in range(IB):
                for a in range(UB):
                    lanes = slice((cc * UB + a) * SIDE, (cc * UB + a + 1) * SIDE)
                    tile = marked[slots[(cc * UB + a) * IB + b], :, c]
                    rates[b * NX * PIECE:(b + 1) * NX * PIECE, lanes] = tile.reshape(NX * PIECE, SIDE)

    def product(t, j, n):
        cc, a = divmod(2 * n, UB)
        return lax.dot_general(
            panel_at(t, j, slice(None)).reshape(NY * NX * PIECE, W),
            users[cc, a:a + 2, :, columns(j)].reshape(2 * SIDE, W),
            (((1,), (1,)), ((), ())), preferred_element_type=F32,
        )

    def group(n):
        return slice(n * 2 * SIDE, (n + 1) * 2 * SIDE)

    def predict_first(t):
        for n in range(UB):
            remaining[n] = rates[:, group(n)].astype(F32) - product(t, 0, n)

    def errors(t):
        for n in range(UB):
            rest = remaining[n]
            dense_t[:, group(n)] = jnp.where(rest < LIMIT, rest - product(t, 1, n), 0.0).astype(BF)

    def user_grad(t, cc, j):
        return lax.dot_general(
            dense_t[:, cc * UB * SIDE:(cc + 1) * UB * SIDE], panel_at(t, j, slice(None)).reshape(NY * NX * PIECE, W),
            (((0,), (0,)), ((), ())), preferred_element_type=F32,
        ).reshape(UB, SIDE, W)

    def send_user_grads(t):
        for j in range(J):
            u_out[t, :, :, columns(j)] = user_grad(t, 1, j).astype(BF)
        user_grads(t).start()
        for j in range(J):
            u_own[:, :, columns(j)] = user_grad(t, 0, j)

    def update_users(t):
        user_grads(t).wait_recv()
        if t > 0:
            new_users(t - 1).wait_send()
        for j in range(J):
            grad = u_own[:, :, columns(j)] + u_in[t, :, :, columns(j)].astype(F32)
            factor = users[0, :, :, columns(j)].astype(F32)
            users[0, :, :, columns(j)] = (factor + step_user * (grad - shrinkage * factor)).astype(BF)

    for i in range(len(PEERS)):
        first_copy(i, y, x).start()
    for n in range(len(pairs)):
        share(n).start()
    marked[2 * K] = jnp.full((NX, NC, PIECE, SIDE), MARK, BF)
    for load in loads:
        load.wait()
    mark(0, 0)
    for n in range(len(pairs)):
        share(n).wait_recv()
    mark(0, 1)
    place(0)
    for i, (dy, dx) in enumerate(PEERS):
        first_copy(i, row(4 - dy), (1 - x if dx else x)).wait_recv()
    predict_first(0)

    for t in range(T):
        errors(t)
        for j in range(J):
            grads[j] = jnp.dot(
                dense_t[...], users[:, :, :, columns(j)].reshape(NC * UB * SIDE, W), preferred_element_type=F32
            ).reshape(NY, NX, PIECE, W)
            for i, (dy, dx) in enumerate(PEERS):
                r_out[t, j, i] = grads[j, row(dy), 1 - x if dx else x].astype(BF)
                reduce(t, j, i).start()
        send_user_grads(t)
        if t == T - 1:
            update_users(t)
            out = pltpu.make_async_copy(users.at[0], users_out, load_sem.at[0])
            out.start()
        for j in range(J):
            reduce_all(t, j).wait_recv()
            total = grads[j, y, x]
            for i in range(len(PEERS)):
                total += r_in[t, j, i].astype(F32)
            mine = panel_at(t, j, y, x).astype(F32) if t else items[:, columns(j)]
            fresh = mine + step_item * (total - shrinkage * mine)
            if t < T - 1:
                a_out[t, j] = fresh.astype(BF)
                for i in range(len(NEXT)):
                    advance(t, j, i).start()
            else:
                items[:, columns(j)] = fresh
        if t < T - 1:
            update_users(t)
            new_users(t).start()
            for cc in range(NC):
                mark(t + 1, cc)
            place(t + 1)
            new_users(t).wait_recv()
            advance_all(t, 0).wait_recv()
            predict_first(t + 1)
            advance_all(t, 1).wait_recv()
        else:
            last = pltpu.make_async_copy(items, items_out, load_sem.at[1])
            last.start()

    for n in range(len(pairs)):
        share(n).wait_send()
    for i in range(len(PEERS)):
        first_copy(i, y, x).wait_send()
    for t in range(T):
        user_grads(t).wait_send()
        for j in range(J):
            reduce_all(t, j).wait_send()
            if t < T - 1:
                for i in range(len(NEXT)):
                    advance(t, j, i).wait_send()
    out.wait()
    last.wait()


def store(users_in, items_in, users_out, items_out, sem):
    copies = [
        pltpu.make_async_copy(users_in, users_out, sem.at[0]),
        pltpu.make_async_copy(items_in, items_out, sem.at[1]),
    ]
    for copy in copies:
        copy.start()
    for copy in copies:
        copy.wait()


def shards(user_factors, item_factors, tile_blocks, tile_counts, ratings, mask_words):
    dma = pltpu.SemaphoreType.DMA
    vmem = pltpu.VMEM
    space = pl.BlockSpec(memory_space=pl.ANY)
    n = len(PEERS)

    def far(a):
        return pltpu.with_memory_space_constraint(a, pltpu.HBM)

    users, panel = pl.pallas_call(
        kernel,
        out_shape=(
            jax.ShapeDtypeStruct((UB, SIDE, R), BF),
            jax.ShapeDtypeStruct((PIECE, R), F32),
        ),
        in_specs=[pl.BlockSpec(memory_space=pltpu.HBM)] * 6,
        out_specs=(space, space),
        scratch_shapes=[
            pltpu.SMEM((NC, T, 2, K), jnp.int32),
            pltpu.SMEM((NC, T), jnp.int32),
            vmem((NC, UB, SIDE, R), BF),
            vmem((PIECE, R), F32),
            vmem((NC, T * K, SIDE, SIDE), BF),
            vmem((NC, T * K, SIDE // 8, SIDE), jnp.int32),
            vmem((NC * K + 1, NX, NC, PIECE, SIDE), BF),
            vmem((NY * NX * PIECE, NC * UB * SIDE), BF),
            vmem((J, NY, NX, PIECE, W), BF),
            [[vmem((NY, NX, PIECE, W), BF) for j in range(J)] for t in range(T - 1)],
            vmem((UB, NY * NX * PIECE, 2 * SIDE), F32),
            vmem((NY * NX * PIECE, NC * UB * SIDE), BF),
            vmem((J, NY, NX, PIECE, W), F32),
            vmem((UB, SIDE, R), F32),
            vmem((T, UB, SIDE, R), BF),
            vmem((T, UB, SIDE, R), BF),
            vmem((T - 1, J, PIECE, W), BF),
            vmem((T, J, n, PIECE, W), BF),
            vmem((T, J, n, PIECE, W), BF),
            dma((6,)),
            dma((5,)), dma((5,)),
            dma((T,)), dma((T,)),
            dma((T - 1,)), dma((T - 1,)),
            dma((T - 1, J, len(NEXT))), dma((T - 1, J)),
            dma((T, J)), dma((T, J)),
            dma((n,)), dma((n,)),
        ],
        compiler_params=pltpu.CompilerParams(
            collective_id=0, has_side_effects=True, vmem_limit_bytes=36 * 1024 * 1024
        ),
    )(
        far(tile_blocks.reshape(T, K, 2).transpose(0, 2, 1)),
        far(tile_counts.reshape(T)),
        far(user_factors.reshape(UB, SIDE, R)),
        far(item_factors),
        far(ratings.reshape(T * K, SIDE, SIDE)),
        far(mask_words.reshape(T * K, SIDE // 8, SIDE)),
    )
    users, panel = pl.pallas_call(
        store,
        out_shape=(
            jax.ShapeDtypeStruct((UB, SIDE, R), BF),
            jax.ShapeDtypeStruct((PIECE, R), F32),
        ),
        in_specs=[space] * 2,
        out_specs=(pl.BlockSpec(memory_space=pltpu.HBM),) * 2,
        scratch_shapes=[dma((2,))],
        compiler_params=pltpu.CompilerParams(vmem_limit_bytes=1024 * 1024),
    )(users, panel)
    return users.reshape(UB * SIDE, R), panel


def solution(mesh):
    placed = (
        P(("strata", "shard"), None),
        P(("strata", "shard"), None),
        P("strata", "shard", None, None, None),
        P("strata", "shard", None),
        P("strata", "shard", None, None, None, None),
        P("strata", "shard", None, None, None, None),
    )
    return jax.shard_map(
        shards,
        mesh=mesh,
        in_specs=placed,
        out_specs=(P(("strata", "shard"), None), P(("strata", "shard"), None)),
        check_vma=False,
    )
```

```python
import jax
import jax.numpy as jnp
from jax import lax
from jax.experimental import pallas as pl
from jax.experimental.pallas import tpu as pltpu
from jax.sharding import PartitionSpec as P

MESH = pl.DeviceIdType.MESH
BF = jnp.bfloat16
F32 = jnp.float32

step_user = 0.05
step_item = 0.004
shrinkage = 0.05

NY, NX, NC = 4, 2, 2
T, K, SIDE, R = 3, 8, 128, 512
J, W = 2, 256
PIECE = 32
UB, IB = 8, 4
N_STRATA = 32
MARK = 1e30
LIMIT = 1e20
PEERS = [(2, 1), (1, 1), (3, 1), (2, 0), (0, 1), (1, 0), (3, 0)]
NEXT = [(2, 1), (2, 0), (1, 1), (1, 0), (3, 1), (3, 0), (0, 1), (0, 0)]


def kernel(
    blocks_in, counts_in, users_in, items_in, ratings_in, words_in,
    users_out, items_out,
    blocks, counts, users, items, ratings, words, marked, rates, panel0, panels, remaining, dense_t, grads,
    u_own, u_out, u_in, a_out, r_out, r_in,
    load_sem, pair_send, pair_recv, u_send, u_recv, n_send, n_recv, a_send, a_recv, r_send, r_recv, i_send, i_recv,
):
    s = lax.axis_index("strata")
    h = lax.axis_index("shard")
    y = h // 4
    x = (h // 2) % 2
    c = h % 2
    after = lax.rem(s + 1, N_STRATA)
    before = lax.rem(s + N_STRATA - 1, N_STRATA)

    def row(dy):
        return lax.rem(y + dy + c * (NY - 2 * dy), NY)

    def at(dy, dx, cc):
        return row(dy) * 4 + (1 - x if dx else x) * 2 + cc

    mate = (s, at(0, 0, 1 - c))

    barrier = pltpu.get_barrier_semaphore()
    partners = [mate] + [(s, at(dy, dx, c)) for dy, dx in PEERS]
    partners += [(after, row(dy) * 4 + xx * 2 + c) for dy, xx in NEXT]
    partners += [(before, row(dy) * 4 + xx * 2 + c) for dy, xx in NEXT]
    for partner in partners:
        pl.semaphore_signal(barrier, inc=1, device_id=partner, device_id_type=MESH)

    first_load = pltpu.make_async_copy(items_in, items, load_sem.at[0])
    first_load.start()
    pairs = [(blocks_in, blocks), (counts_in, counts), (ratings_in, ratings), (words_in, words), (users_in, users)]
    loads = [pltpu.make_async_copy(src, dst.at[0], load_sem.at[n + 1]) for n, (src, dst) in enumerate(pairs)]
    for load in loads:
        load.start()

    first_load.wait()
    for j in range(J):
        panel0[j, y, x] = items[:, j * W:(j + 1) * W].astype(BF)

    pl.semaphore_wait(barrier, len(partners))

    def remote(src, dst, send, recv, to):
        return pltpu.make_async_remote_copy(
            src_ref=src, dst_ref=dst, send_sem=send, recv_sem=recv, device_id=to, device_id_type=MESH
        )

    def panel_at(t, j, *index):
        return panels[t - 1][j][index] if t else panel0[(j, *index)]

    def first_copy(i, yy, xx):
        part = panel0.at[:, yy, xx]
        dy, dx = PEERS[i]
        return remote(part, part, i_send.at[i], i_recv.at[i], (s, at(dy, dx, c)))

    def share(n):
        src, dst = pairs[n]
        return remote(src, dst.at[1], pair_send.at[n], pair_recv.at[n], mate)

    def reduce(t, j, i):
        dy, dx = PEERS[i]
        return remote(r_out.at[t, j, i], r_in.at[t, j, i], r_send.at[t, j], r_recv.at[t, j], (s, at(dy, dx, c)))

    def reduce_all(t, j):
        return remote(r_out.at[t, j], r_in.at[t, j], r_send.at[t, j], r_recv.at[t, j], mate)

    def advance(t, j, i):
        dy, xx = NEXT[i]
        return remote(
            a_out.at[t, j], panels[t][j].at[y, x], a_send.at[t, j, i], a_recv.at[t, j],
            (after, row(dy) * 4 + xx * 2 + c),
        )

    def advance_all(t, j):
        return remote(panels[t][j], panels[t][j], a_send.at[t, j, 0], a_recv.at[t, j], mate)

    def user_grads(t):
        return remote(u_out.at[t], u_in.at[t], u_send.at[t], u_recv.at[t], mate)

    def new_users(t):
        return remote(users.at[0], users.at[1], n_send.at[t], n_recv.at[t], mate)

    def columns(j):
        return slice(j * W, (j + 1) * W)

    bit = lax.broadcasted_iota(jnp.int32, (16, 8, SIDE), 1)

    def mark(t, cc):
        for k in range(K):
            live = (k < counts[cc, t]).astype(jnp.int32)
            mask = jnp.bitwise_and(jnp.right_shift(words[cc, t * K + k][:, None, :], bit), live).reshape(SIDE, SIDE)
            rate = jnp.where(mask != 0, ratings[cc, t * K + k].astype(F32), MARK)
            marked[cc * K + k] = rate.T.astype(BF).reshape(NX, NC, PIECE, SIDE)

    def slots_of(t):
        found = []
        for cc in range(NC):
            cells = [blocks[cc, t, 0, k] * IB + blocks[cc, t, 1, k] for k in range(K)]
            for cell in range(UB * IB):
                rank = (cells[0] == cell).astype(jnp.int32) * (2 * K - cc * K)
                for k in range(1, K):
                    rank = jnp.maximum(rank, (cells[k] == cell).astype(jnp.int32) * (2 * K - cc * K - k))
                found.append(2 * K - rank)
        return found

    def place(t):
        slots = slots_of(t)
        for cc in range(NC):
            for b in range(IB):
                for a in range(UB):
                    lanes = slice((cc * UB + a) * SIDE, (cc * UB + a + 1) * SIDE)
                    tile = marked[slots[(cc * UB + a) * IB + b], :, c]
                    rates[b * NX * PIECE:(b + 1) * NX * PIECE, lanes] = tile.reshape(NX * PIECE, SIDE)

    def product(t, j, n):
        cc, a = divmod(2 * n, UB)
        return lax.dot_general(
            panel_at(t, j, slice(None)).reshape(NY * NX * PIECE, W),
            users[cc, a:a + 2, :, columns(j)].reshape(2 * SIDE, W),
            (((1,), (1,)), ((), ())), preferred_element_type=F32,
        )

    def group(n):
        return slice(n * 2 * SIDE, (n + 1) * 2 * SIDE)

    def predict_first(t):
        for n in range(UB):
            remaining[n] = rates[:, group(n)].astype(F32) - product(t, 0, n)

    def errors(t):
        for n in range(UB):
            rest = remaining[n]
            dense_t[:, group(n)] = jnp.where(rest < LIMIT, rest - product(t, 1, n), 0.0).astype(BF)

    def user_grad(t, cc, j):
        return lax.dot_general(
            dense_t[:, cc * UB * SIDE:(cc + 1) * UB * SIDE], panel_at(t, j, slice(None)).reshape(NY * NX * PIECE, W),
            (((0,), (0,)), ((), ())), preferred_element_type=F32,
        ).reshape(UB, SIDE, W)

    def send_user_grads(t):
        for j in range(J):
            u_out[t, :, :, columns(j)] = user_grad(t, 1, j).astype(BF)
        user_grads(t).start()
        for j in range(J):
            u_own[:, :, columns(j)] = user_grad(t, 0, j)

    def update_users(t):
        user_grads(t).wait_recv()
        if t > 0:
            new_users(t - 1).wait_send()
        for j in range(J):
            grad = u_own[:, :, columns(j)] + u_in[t, :, :, columns(j)].astype(F32)
            factor = users[0, :, :, columns(j)].astype(F32)
            users[0, :, :, columns(j)] = (factor + step_user * (grad - shrinkage * factor)).astype(BF)

    for i in range(len(PEERS)):
        first_copy(i, y, x).start()
    for n in range(len(pairs)):
        share(n).start()
    marked[2 * K] = jnp.full((NX, NC, PIECE, SIDE), MARK, BF)
    for load in loads:
        load.wait()
    mark(0, 0)
    for n in range(len(pairs) - 1):
        share(n).wait_recv()
    mark(0, 1)
    place(0)
    share(len(pairs) - 1).wait_recv()
    for i, (dy, dx) in enumerate(PEERS):
        first_copy(i, row(4 - dy), (1 - x if dx else x)).wait_recv()
    predict_first(0)

    for t in range(T):
        errors(t)
        for j in range(J):
            grads[j] = jnp.dot(
                dense_t[...], users[:, :, :, columns(j)].reshape(NC * UB * SIDE, W), preferred_element_type=F32
            ).reshape(NY, NX, PIECE, W)
            for i, (dy, dx) in enumerate(PEERS):
                r_out[t, j, i] = grads[j, row(dy), 1 - x if dx else x].astype(BF)
                reduce(t, j, i).start()
        send_user_grads(t)
        if t == T - 1:
            update_users(t)
            out = pltpu.make_async_copy(users.at[0], users_out, load_sem.at[0])
            out.start()
        for j in range(J):
            reduce_all(t, j).wait_recv()
            total = grads[j, y, x]
            for i in range(len(PEERS)):
                total += r_in[t, j, i].astype(F32)
            mine = panel_at(t, j, y, x).astype(F32) if t else items[:, columns(j)]
            fresh = mine + step_item * (total - shrinkage * mine)
            if t < T - 1:
                a_out[t, j] = fresh.astype(BF)
                for i in range(len(NEXT)):
                    advance(t, j, i).start()
            else:
                items[:, columns(j)] = fresh
        if t < T - 1:
            update_users(t)
            new_users(t).start()
            for cc in range(NC):
                mark(t + 1, cc)
            place(t + 1)
            new_users(t).wait_recv()
            advance_all(t, 0).wait_recv()
            predict_first(t + 1)
            advance_all(t, 1).wait_recv()
        else:
            last = pltpu.make_async_copy(items, items_out, load_sem.at[1])
            last.start()

    for n in range(len(pairs)):
        share(n).wait_send()
    for i in range(len(PEERS)):
        first_copy(i, y, x).wait_send()
    for t in range(T):
        user_grads(t).wait_send()
        for j in range(J):
            reduce_all(t, j).wait_send()
            if t < T - 1:
                for i in range(len(NEXT)):
                    advance(t, j, i).wait_send()
    out.wait()
    last.wait()


def store(users_in, items_in, users_out, items_out, sem):
    copies = [pltpu.make_async_copy(items_in, items_out, sem.at[0])]
    for n in range(4):
        part = pl.ds(n * UB // 4, UB // 4)
        copies.append(pltpu.make_async_copy(users_in.at[part], users_out.at[part], sem.at[n + 1]))
    for copy in copies:
        copy.start()
    for copy in copies:
        copy.wait()


def shards(user_factors, item_factors, tile_blocks, tile_counts, ratings, mask_words):
    dma = pltpu.SemaphoreType.DMA
    vmem = pltpu.VMEM
    space = pl.BlockSpec(memory_space=pl.ANY)
    n = len(PEERS)

    def far(a):
        return pltpu.with_memory_space_constraint(a, pltpu.HBM)

    users, panel = pl.pallas_call(
        kernel,
        out_shape=(
            jax.ShapeDtypeStruct((UB, SIDE, R), BF),
            jax.ShapeDtypeStruct((PIECE, R), F32),
        ),
        in_specs=[pl.BlockSpec(memory_space=pltpu.HBM)] * 6,
        out_specs=(space, space),
        scratch_shapes=[
            pltpu.SMEM((NC, T, 2, K), jnp.int32),
            pltpu.SMEM((NC, T), jnp.int32),
            vmem((NC, UB, SIDE, R), BF),
            vmem((PIECE, R), F32),
            vmem((NC, T * K, SIDE, SIDE), BF),
            vmem((NC, T * K, SIDE // 8, SIDE), jnp.int32),
            vmem((NC * K + 1, NX, NC, PIECE, SIDE), BF),
            vmem((NY * NX * PIECE, NC * UB * SIDE), BF),
            vmem((J, NY, NX, PIECE, W), BF),
            [[vmem((NY, NX, PIECE, W), BF) for j in range(J)] for t in range(T - 1)],
            vmem((UB, NY * NX * PIECE, 2 * SIDE), F32),
            vmem((NY * NX * PIECE, NC * UB * SIDE), BF),
            vmem((J, NY, NX, PIECE, W), F32),
            vmem((UB, SIDE, R), F32),
            vmem((T, UB, SIDE, R), BF),
            vmem((T, UB, SIDE, R), BF),
            vmem((T - 1, J, PIECE, W), BF),
            vmem((T, J, n, PIECE, W), BF),
            vmem((T, J, n, PIECE, W), BF),
            dma((6,)),
            dma((5,)), dma((5,)),
            dma((T,)), dma((T,)),
            dma((T - 1,)), dma((T - 1,)),
            dma((T - 1, J, len(NEXT))), dma((T - 1, J)),
            dma((T, J)), dma((T, J)),
            dma((n,)), dma((n,)),
        ],
        compiler_params=pltpu.CompilerParams(
            collective_id=0, has_side_effects=True, vmem_limit_bytes=36 * 1024 * 1024
        ),
    )(
        far(tile_blocks.reshape(T, K, 2).transpose(0, 2, 1)),
        far(tile_counts.reshape(T)),
        far(user_factors.reshape(UB, SIDE, R)),
        far(item_factors),
        far(ratings.reshape(T * K, SIDE, SIDE)),
        far(mask_words.reshape(T * K, SIDE // 8, SIDE)),
    )
    users, panel = pl.pallas_call(
        store,
        out_shape=(
            jax.ShapeDtypeStruct((UB, SIDE, R), BF),
            jax.ShapeDtypeStruct((PIECE, R), F32),
        ),
        in_specs=[space] * 2,
        out_specs=(pl.BlockSpec(memory_space=pltpu.HBM),) * 2,
        scratch_shapes=[dma((5,))],
        compiler_params=pltpu.CompilerParams(vmem_limit_bytes=1024 * 1024),
    )(users, panel)
    return users.reshape(UB * SIDE, R), panel


def solution(mesh):
    placed = (
        P(("strata", "shard"), None),
        P(("strata", "shard"), None),
        P("strata", "shard", None, None, None),
        P("strata", "shard", None),
        P("strata", "shard", None, None, None, None),
        P("strata", "shard", None, None, None, None),
    )
    return jax.shard_map(
        shards,
        mesh=mesh,
        in_specs=placed,
        out_specs=(P(("strata", "shard"), None), P(("strata", "shard"), None)),
        check_vma=False,
    )
```
